512 devices in a mesh: ctx: 64 (over z_hi, x, y, core), kvh: 8 (over z_lo).
Axes of the slice: x: 4, y: 4, z: 16 (z_hi: 2, z_lo: 8; z = z_hi * 8 + z_lo), core: 2. Of those that a mesh axis runs over, the one named last changes fastest.
Arguments:
- doc_lengths: int32 [33], replicated, may hold values from 1 to 896, 16384 in all
- queries: bfloat16 [16384, 4096], P('ctx', 'kvh'), may hold values from -6 to 6
- keys: bfloat16 [16384, 1024], P('ctx', 'kvh'), may hold values from -6 to 6
- values: bfloat16 [16384, 1024], P('ctx', 'kvh'), may hold values from -12 to 12
- o_weight: bfloat16 [4096, 4096], P('kvh'), may hold values from -0.09375 to 0.09375
Outputs:
- projected: bfloat16 [16384, 4096], P(('ctx', 'kvh'))
The draws below stay inside these ranges and needn't reach their ends.
Inputs may be any that keep to these rules, and one draw needn't show every extreme that they name: `doc_lengths`: the documents in sequence order; they sum to 16384.
All inputs are finite; a program needn't handle non-finite values.
Results may differ from the reference program's by a relative error of at most 0.018.
Values may be sent and summed in bfloat16 or wider, within the bound.
No kernel may reach another device: no remote copies, remote signals or barrier semaphores. Data moves between devices by JAX's collectives and lax.ppermute only.
A program may use at most 64 MiB of HBM per device.

```python
import math
import jax
import jax.numpy as jnp
import numpy as np
from jax import lax

D = 4096
HEAD_WIDTH = 128
QUERY_PER_KEY = 4
KEY_HEADS = 8
HQ = 32
TOK_DEV = 256
STRETCH = 128
PACKED_LENGTH = 16384
DOCUMENT_LIMIT = 896
NDOCS = 33
N_KVH = 8


def draw_queries(key, part):
    sampled_tensors = jax.random.truncated_normal(jax.random.fold_in(key, 11), -6.0, 6.0, (PACKED_LENGTH, KEY_HEADS, QUERY_PER_KEY, HEAD_WIDTH), jnp.float32)
    return sampled_tensors.reshape(PACKED_LENGTH, HQ * HEAD_WIDTH).astype(jnp.bfloat16)


def draw_keys(key, part):
    sampled_tensors = jax.random.truncated_normal(jax.random.fold_in(key, 12), -6.0, 6.0, (PACKED_LENGTH, KEY_HEADS, HEAD_WIDTH), jnp.float32)
    return sampled_tensors.reshape(PACKED_LENGTH, KEY_HEADS * HEAD_WIDTH).astype(jnp.bfloat16)


def draw_values(key, part):
    sampled_tensors = jax.random.truncated_normal(jax.random.fold_in(key, 13), -4.0, 4.0, (PACKED_LENGTH, KEY_HEADS * HEAD_WIDTH), jnp.float32)
    row_scale = jnp.exp(jax.random.uniform(jax.random.fold_in(key, 14), (PACKED_LENGTH,), jnp.float32, math.log(0.3), math.log(3.0)))
    return (sampled_tensors * row_scale[:, None]).astype(jnp.bfloat16)


def shard_levels(stream_key, shape, shards, smallest, top_value):
    gain, own = 1.0, jax.random.fold_in(stream_key, 6)
    for dim, parts in shards:
        heights = jnp.exp(jax.random.uniform(jax.random.fold_in(own, dim), (parts,), jnp.float32, smallest / len(shards), top_value / len(shards)))
        gain = gain * jnp.repeat(heights, shape[dim] // parts).reshape([-1 if axis == dim else 1 for axis in range(len(shape))])
    return gain


def profile(number_of, total, bound, skew):
    weights = [(1 << 20) // math.isqrt(grade ** skew) + 1 for grade in range(2, number_of + 1)]
    surplus, holding = total - bound - (number_of - 1), [1] * (number_of - 1)
    while surplus > 0:
        candidates = [i for i in range(number_of - 1) if holding[i] < bound]
        pool, left = sum([weights[i] for i in candidates]), surplus
        for i in candidates:
            more = min(bound - holding[i], max(1, left * weights[i] // pool), surplus)
            holding[i] = holding[i] + more
            surplus = surplus - more
    return np.array([bound] + holding)


def ragged(rng, number_of, total, bound, skew):
    if number_of == 2:
        one = jax.random.randint(rng, (), max(1, total - bound), min(bound, total - 1) + 1)
        return jnp.stack([one, total - one])
    sizes = jnp.asarray(profile(number_of, total, bound, skew), jnp.int32)
    twos = (number_of - 1) // 2
    giver, taker = sizes[1:1 + 2 * twos:2], sizes[2:2 + 2 * twos:2]
    slack = jnp.minimum(giver - 1, bound - taker)
    shifted = jax.random.randint(jax.random.fold_in(rng, 1), (twos,), 0, 1 << 20) % (slack + 1)
    sizes = sizes.at[1:1 + 2 * twos:2].set(giver - shifted).at[2:2 + 2 * twos:2].set(taker + shifted)
    return sizes[jax.random.permutation(jax.random.fold_in(rng, 2), number_of)]


def normal_values(key, shape, deviation, reach, shards=(), held_as=jnp.bfloat16):
    level = shard_levels(key, shape, shards, -0.22, 0.18) if shards else 1.0
    array = jax.random.normal(key, shape, jnp.float32) * deviation * level
    return jnp.minimum(jnp.maximum(array, -reach), reach).astype(held_as)


def setup_inputs(seed: int = 0) -> dict:
    key_list = jax.random.split(jax.random.key(seed), 6)
    doc_lengths = ragged(key_list[0], NDOCS, PACKED_LENGTH, DOCUMENT_LIMIT, 1).astype(jnp.int32)
    queries = draw_queries(jax.random.fold_in(key_list[5], 71), 0)
    keys = draw_keys(jax.random.fold_in(key_list[5], 71), 0)
    values = draw_values(jax.random.fold_in(key_list[5], 71), 0)
    o_weight = normal_values(key_list[4], (HQ * HEAD_WIDTH, D), (HQ * HEAD_WIDTH) ** -0.5, 0.09375, ((0, 8),))
    return {"doc_lengths": doc_lengths, "queries": queries, "keys": keys, "values": values, "o_weight": o_weight}


NEG_FILL = -1e+30

def reference(doc_lengths, queries, keys, values, o_weight):
    row_ids = jnp.arange(PACKED_LENGTH, dtype=jnp.int32)
    source_index = row_ids // TOK_DEV
    offset_rows = row_ids % TOK_DEV
    places = jnp.where(offset_rows < STRETCH, source_index * STRETCH + offset_rows, PACKED_LENGTH - (source_index + 2) * STRETCH + offset_rows).astype(jnp.int32)
    plain_layout = jnp.zeros((PACKED_LENGTH,), jnp.int32).at[places].set(row_ids)
    doc_ends = jnp.cumsum(doc_lengths).astype(jnp.int32)
    documents = lax.optimization_barrier(jnp.sum((doc_ends[None, :] <= row_ids[:, None]).astype(jnp.int32), axis=1)).astype(jnp.int32)
    query_plain = queries[plain_layout].reshape(PACKED_LENGTH, KEY_HEADS, QUERY_PER_KEY, HEAD_WIDTH)
    key_plain = keys[plain_layout].reshape(PACKED_LENGTH, KEY_HEADS, HEAD_WIDTH)
    value_plain = values[plain_layout].reshape(PACKED_LENGTH, KEY_HEADS, HEAD_WIDTH)
    key_padded = jnp.concatenate([jnp.zeros((DOCUMENT_LIMIT, KEY_HEADS, HEAD_WIDTH), key_plain.dtype), key_plain], axis=0)
    value_padded = jnp.concatenate([jnp.zeros((DOCUMENT_LIMIT, KEY_HEADS, HEAD_WIDTH), value_plain.dtype), value_plain], axis=0)
    doc_pad = jnp.concatenate([jnp.full((DOCUMENT_LIMIT,), -1, jnp.int32), documents], axis=0)
    scaling = 1.0 / math.sqrt(HEAD_WIDTH)

    def one_block(block_index):
        first_row = (block_index * STRETCH).astype(jnp.int32)
        query_part = lax.dynamic_slice_in_dim(query_plain, first_row, STRETCH, 0).astype(jnp.float32)
        key_part = lax.dynamic_slice_in_dim(key_padded, first_row, STRETCH + DOCUMENT_LIMIT, 0).astype(jnp.float32)
        value_part = lax.dynamic_slice_in_dim(value_padded, first_row, STRETCH + DOCUMENT_LIMIT, 0).astype(jnp.float32)
        key_docs = lax.dynamic_slice_in_dim(doc_pad, first_row, STRETCH + DOCUMENT_LIMIT, 0)
        query_docs = lax.dynamic_slice_in_dim(documents, first_row, STRETCH, 0)
        query_places = first_row + jnp.arange(STRETCH, dtype=jnp.int32)
        key_places = first_row - DOCUMENT_LIMIT + jnp.arange(STRETCH + DOCUMENT_LIMIT, dtype=jnp.int32)
        allowed = (key_docs[None, :] == query_docs[:, None]) & (key_places[None, :] <= query_places[:, None])
        scores = jnp.einsum('cgjd,kgd->cgjk', query_part, key_part) * scaling
        scores = jnp.where(allowed[:, None, None, :], scores, NEG_FILL)
        highest = lax.optimization_barrier(jnp.max(scores, axis=3, keepdims=True))
        weights = jnp.where(allowed[:, None, None, :], jnp.exp(scores - highest), 0.0)
        weights = weights / lax.optimization_barrier(jnp.sum(weights, axis=3, keepdims=True))
        weights = lax.optimization_barrier(weights.astype(jnp.bfloat16)).astype(jnp.float32)
        result = jnp.einsum('cgjk,kgd->cgjd', weights, value_part)
        return result.reshape(STRETCH, HQ * HEAD_WIDTH).astype(jnp.bfloat16)
    blocks_nat = lax.map(one_block, jnp.arange(PACKED_LENGTH // STRETCH, dtype=jnp.int32)).reshape(PACKED_LENGTH, HQ * HEAD_WIDTH)
    attention = blocks_nat[places]
    grouped = attention.reshape(PACKED_LENGTH, N_KVH, HQ * HEAD_WIDTH // N_KVH)
    weight_groups = o_weight.reshape(N_KVH, HQ * HEAD_WIDTH // N_KVH, D)
    summed = jnp.zeros((PACKED_LENGTH, D), jnp.float32)
    for group in range(N_KVH):
        partial_value = jnp.dot(grouped[:, group], weight_groups[group], preferred_element_type=jnp.float32).astype(jnp.bfloat16)
        partial_value = lax.optimization_barrier(partial_value)
        summed = summed + partial_value.astype(jnp.float32)
    return summed.astype(jnp.bfloat16)
```

```python
import math

import jax
import jax.numpy as jnp
from jax import lax
from jax.experimental import pallas as pl
from jax.experimental.pallas import tpu as pltpu
from jax.sharding import PartitionSpec as P

BF = jnp.bfloat16
F32 = jnp.float32
HEAD_WIDTH = 128
STRETCH = 128
GROUP = 8
NEG_FILL = -1e30
SCALE = math.log2(math.e) / math.sqrt(HEAD_WIDTH)
VMEM = pl.BlockSpec(memory_space=pltpu.VMEM)
SMEM = pl.BlockSpec(memory_space=pltpu.SMEM)


def prep_kernel(k_ref, v_ref, low_ref, high_ref, own_ref):
    me = lax.rem(lax.axis_index("ctx"), GROUP)
    low_ref[:STRETCH] = k_ref[:STRETCH]
    low_ref[STRETCH:] = v_ref[:STRETCH]
    high_ref[:STRETCH] = k_ref[STRETCH:]
    high_ref[STRETCH:] = v_ref[STRETCH:]
    for j in range(GROUP):
        @pl.when(j >= me)
        def _():
            own_ref[j] = low_ref[...]

        @pl.when(j < me)
        def _():
            own_ref[j] = high_ref[...]


def pass_kernel(groups, low_ref, high_ref, mirror_ref, out_ref):
    ctx = lax.axis_index("ctx")
    me = lax.rem(ctx, GROUP)
    last = ctx >= (groups - 1) * GROUP
    for j in range(GROUP):
        @pl.when((j >= me) & last)
        def _():
            out_ref[j] = mirror_ref[...]

        @pl.when((j >= me) & jnp.logical_not(last))
        def _():
            out_ref[j] = high_ref[...]

        @pl.when(j < me)
        def _():
            out_ref[j] = low_ref[...]


def main_kernel(stretches, docs, q_ref, k_ref, v_ref, own_ref, sh_ref, len_ref, w_hbm, *rest):
    outs, (kbuf, vbuf, bias, attn, rows, wbuf, sem) = rest[:8], rest[8:]
    ctx = lax.axis_index("ctx")
    kvh = lax.axis_index("kvh")
    me = lax.rem(ctx, GROUP)
    group0 = ctx - me
    copy = pltpu.make_async_copy(w_hbm, wbuf, sem)
    copy.start()
    heads = q_ref.shape[1] // HEAD_WIDTH
    row = lax.broadcasted_iota(jnp.int32, (STRETCH, HEAD_WIDTH), 0)
    lane = lax.broadcasted_iota(jnp.int32, (STRETCH, HEAD_WIDTH), 1)
    for chain in range(2):
        q_base = (ctx if chain == 0 else stretches - 1 - ctx) * STRETCH
        q_place = q_base + row
        begin = jnp.zeros_like(row)
        end = jnp.int32(0)
        for n in range(docs):
            end = end + len_ref[n]
            begin = jnp.where(end <= q_place, end, begin)
        for s in range(GROUP):
            here = pl.ds(s * STRETCH, STRETCH)
            if chain == 0:
                near = s <= me
                source = group0 + s - jnp.where(near, 0, GROUP)
                key_base = source * STRETCH
            else:
                near = s >= me
                source = group0 + s + jnp.where(near, 0, GROUP)
                key_base = (stretches - 1 - source) * STRETCH

            @pl.when(near)
            def _():
                kbuf[here] = own_ref[s, :STRETCH]
                vbuf[here] = own_ref[s, STRETCH:]

            @pl.when(jnp.logical_not(near))
            def _():
                kbuf[here] = sh_ref[s, :STRETCH]
                vbuf[here] = sh_ref[s, STRETCH:]

            if chain == 1:
                @pl.when(s == me)
                def _():
                    kbuf[here] = k_ref[STRETCH:]
                    vbuf[here] = v_ref[STRETCH:]

            key_place = key_base + lane
            allowed = (key_place >= begin) & (key_place <= q_place)
            bias[:, here] = jnp.where(allowed, 0.0, NEG_FILL)
        mine = pl.ds(chain * STRETCH, STRETCH)
        for h in range(heads):
            columns = pl.ds(h * HEAD_WIDTH, HEAD_WIDTH)
            scores = lax.dot_general(
                q_ref[mine, columns], kbuf[...], (((1,), (1,)), ((), ())), preferred_element_type=F32
            )
            scores = scores * SCALE + bias[...]
            highest = jnp.max(scores, axis=1, keepdims=True)
            weights = jnp.exp2(scores - highest)
            total = jnp.sum(weights, axis=1, keepdims=True)
            result = jnp.dot(weights.astype(BF), vbuf[...], preferred_element_type=F32)
            attn[mine, columns] = (result / total).astype(BF)
    n_kvh = len(outs)
    chunk = attn.shape[0] // n_kvh
    position = jnp.where(lax.rem(kvh, 2) == 0, kvh // 2, n_kvh - 1 - kvh // 2)
    for o in range(n_kvh):
        i = lax.rem(position + o, n_kvh)
        to = jnp.where(i < n_kvh // 2, 2 * i, 2 * n_kvh - 1 - 2 * i)
        rows[pl.ds(o * chunk, chunk)] = attn[pl.ds(pl.multiple_of(to * chunk, chunk), chunk)]
    copy.wait()
    width = 512
    for c in range(wbuf.shape[1] // width):
        columns = pl.ds(c * width, width)
        part = jnp.dot(rows[...], wbuf[:, columns], preferred_element_type=F32).astype(BF)
        for o in range(n_kvh):
            outs[o][:, columns] = part[o * chunk : (o + 1) * chunk]


def local(doc_lengths, queries, keys, values, o_weight):
    n_ctx = lax.axis_size("ctx")
    n_kvh = lax.axis_size("kvh")
    groups = n_ctx // GROUP
    pair = jax.ShapeDtypeStruct((2 * STRETCH, HEAD_WIDTH), BF)
    eight = jax.ShapeDtypeStruct((GROUP, 2 * STRETCH, HEAD_WIDTH), BF)
    low, high, own = pl.pallas_call(
        prep_kernel, out_shape=(pair, pair, eight), in_specs=[VMEM] * 2, out_specs=(VMEM,) * 3, name="prep"
    )(keys, values)
    top = n_ctx - GROUP
    mirror = lax.ppermute(low, "ctx", [(top + m, n_ctx - 1 - m) for m in range(GROUP)])
    low_in = lax.ppermute(low, "ctx", [(i, i + GROUP) for i in range(n_ctx - GROUP)])
    high_in = lax.ppermute(high, "ctx", [(i, i - GROUP) for i in range(GROUP, n_ctx)])
    members = [list(range(g * GROUP, (g + 1) * GROUP)) for g in range(groups)]

    def exchange(x):
        return lax.all_to_all(x, "ctx", 0, 0, axis_index_groups=members, tiled=True)

    own = exchange(own)
    passed = pl.pallas_call(
        lambda *refs: pass_kernel(groups, *refs),
        out_shape=eight,
        in_specs=[VMEM] * 3,
        out_specs=VMEM,
        name="pass",
    )(low_in, high_in, mirror)
    passed = exchange(passed)
    rows, inner = queries.shape
    width = o_weight.shape[1]
    keys_all = GROUP * STRETCH
    chunk = jax.ShapeDtypeStruct((rows // n_kvh, width), BF)
    part = pl.pallas_call(
        lambda *refs: main_kernel(2 * n_ctx, doc_lengths.shape[0], *refs),
        out_shape=(chunk,) * n_kvh,
        in_specs=[VMEM] * 5 + [SMEM, pl.BlockSpec(memory_space=pl.ANY)],
        out_specs=(VMEM,) * n_kvh,
        scratch_shapes=[
            pltpu.VMEM((keys_all, HEAD_WIDTH), BF),
            pltpu.VMEM((keys_all, HEAD_WIDTH), BF),
            pltpu.VMEM((STRETCH, keys_all), F32),
            pltpu.VMEM((rows, inner), BF),
            pltpu.VMEM((rows, inner), BF),
            pltpu.VMEM(o_weight.shape, BF),
            pltpu.SemaphoreType.DMA,
        ],
        name="attend",
    )(queries, keys, values, own, passed, doc_lengths, o_weight)

    ring = list(range(0, n_kvh, 2)) + list(range(n_kvh - 1, 0, -2))
    onward = [(ring[i], ring[(i + 1) % n_kvh]) for i in range(n_kvh)]
    back = [(to, source) for source, to in onward]

    def add(a, b):
        return (a.astype(F32) + b.astype(F32)).astype(BF)

    a, b = part[n_kvh // 2], part[n_kvh // 2 + 1]
    for distance in range(n_kvh // 2, 1, -1):
        a = add(part[distance - 1], lax.ppermute(a, "kvh", onward))
        b = lax.ppermute(b, "kvh", back)
        if distance > 2:
            b = add(part[n_kvh + 2 - distance], b)
            a, b = lax.optimization_barrier((a, b))
    a = lax.ppermute(a, "kvh", onward)
    return (part[0].astype(F32) + a.astype(F32) + b.astype(F32)).astype(BF)


def solution(mesh):
    in_specs = (P(), P("ctx", "kvh"), P("ctx", "kvh"), P("ctx", "kvh"), P("kvh", None))
    out_specs = P(("ctx", "kvh"), None)
    return jax.shard_map(local, mesh=mesh, in_specs=in_specs, out_specs=out_specs, check_vma=False)
```

```python
import math

import jax
import jax.numpy as jnp
from jax import lax
from jax.experimental import pallas as pl
from jax.experimental.pallas import tpu as pltpu
from jax.sharding import PartitionSpec as P


BF = jnp.bfloat16
F32 = jnp.float32
HEAD_WIDTH = 128
STRETCH = 128
GROUP = 8
NEG_FILL = -1e30
SCALE = math.log2(math.e) / math.sqrt(HEAD_WIDTH)
VMEM = pl.BlockSpec(memory_space=pltpu.VMEM)
SMEM = pl.BlockSpec(memory_space=pltpu.SMEM)


def prep_kernel(k_ref, v_ref, even_ref, odd_ref, own_ref):
    ctx = lax.axis_index("ctx")
    me = lax.rem(ctx, GROUP)
    is_odd = lax.rem(ctx // GROUP, 2) == 1

    def put(ref, at):
        ref[:STRETCH] = k_ref[at : at + STRETCH]
        ref[STRETCH:] = v_ref[at : at + STRETCH]

    @pl.when(is_odd)
    def _():
        put(odd_ref, 0)
        put(even_ref, STRETCH)

    @pl.when(jnp.logical_not(is_odd))
    def _():
        put(odd_ref, STRETCH)
        put(even_ref, 0)

    for j in range(GROUP):

        @pl.when(j >= me)
        def _():
            put(own_ref.at[j], 0)

        @pl.when(j < me)
        def _():
            put(own_ref.at[j], STRETCH)


def pass_kernel(even_ref, odd_ref, out_ref):
    ctx = lax.axis_index("ctx")
    me = lax.rem(ctx, GROUP)
    is_odd = lax.rem(ctx // GROUP, 2) == 1
    for j in range(GROUP):
        from_odd = (j >= me) == is_odd

        @pl.when(from_odd)
        def _():
            out_ref[j] = odd_ref[...]

        @pl.when(jnp.logical_not(from_odd))
        def _():
            out_ref[j] = even_ref[...]


def main_kernel(stretches, docs, q_ref, k_ref, v_ref, own_ref, sh_ref, len_ref, w_hbm, *rest):
    outs, (kbuf, vbuf, bias, attn, rows, wbuf, sem) = rest[:8], rest[8:]
    ctx = lax.axis_index("ctx")
    kvh = lax.axis_index("kvh")
    me = lax.rem(ctx, GROUP)
    group0 = ctx - me
    copy = pltpu.make_async_copy(w_hbm, wbuf, sem)
    copy.start()
    heads = q_ref.shape[1] // HEAD_WIDTH
    row = lax.broadcasted_iota(jnp.int32, (STRETCH, HEAD_WIDTH), 0)
    lane = lax.broadcasted_iota(jnp.int32, (STRETCH, HEAD_WIDTH), 1)
    for chain in range(2):
        q_base = (ctx if chain == 0 else stretches - 1 - ctx) * STRETCH
        q_place = q_base + row
        begin = jnp.zeros_like(row)
        end = jnp.int32(0)
        for n in range(docs):
            end = end + len_ref[n]
            begin = jnp.where(end <= q_place, end, begin)
        for s in range(GROUP):
            here = pl.ds(s * STRETCH, STRETCH)
            if chain == 0:
                near = s <= me
                source = group0 + s - jnp.where(near, 0, GROUP)
                key_base = source * STRETCH
            else:
                near = s >= me
                source = group0 + s + jnp.where(near, 0, GROUP)
                key_base = (stretches - 1 - source) * STRETCH

            @pl.when(near)
            def _():
                kbuf[here] = own_ref[s, :STRETCH]
                vbuf[here] = own_ref[s, STRETCH:]

            @pl.when(jnp.logical_not(near))
            def _():
                kbuf[here] = sh_ref[s, :STRETCH]
                vbuf[here] = sh_ref[s, STRETCH:]

            if chain == 1:
                @pl.when(s == me)
                def _():
                    kbuf[here] = k_ref[STRETCH:]
                    vbuf[here] = v_ref[STRETCH:]

            key_place = key_base + lane
            allowed = (key_place >= begin) & (key_place <= q_place)
            bias[:, here] = jnp.where(allowed, 0.0, NEG_FILL)
        mine = pl.ds(chain * STRETCH, STRETCH)
        for h in range(heads):
            columns = pl.ds(h * HEAD_WIDTH, HEAD_WIDTH)
            scores = lax.dot_general(
                q_ref[mine, columns], kbuf[...], (((1,), (1,)), ((), ())), preferred_element_type=F32
            )
            scores = scores * SCALE + bias[...]
            highest = jnp.max(scores, axis=1, keepdims=True)
            weights = jnp.exp2(scores - highest)
            total = jnp.sum(weights, axis=1, keepdims=True)
            result = jnp.dot(weights.astype(BF), vbuf[...], preferred_element_type=F32)
            attn[mine, columns] = (result / total).astype(BF)
    n_kvh = len(outs)
    chunk = attn.shape[0] // n_kvh
    position = jnp.where(lax.rem(kvh, 2) == 0, kvh // 2, n_kvh - 1 - kvh // 2)
    for o in range(n_kvh):
        i = lax.rem(position + o, n_kvh)
        to = jnp.where(i < n_kvh // 2, 2 * i, 2 * n_kvh - 1 - 2 * i)
        rows[pl.ds(o * chunk, chunk)] = attn[pl.ds(pl.multiple_of(to * chunk, chunk), chunk)]
    copy.wait()
    width = 512
    for c in range(wbuf.shape[1] // width):
        columns = pl.ds(c * width, width)
        part = jnp.dot(rows[...], wbuf[:, columns], preferred_element_type=F32).astype(BF)
        for o in range(n_kvh):
            outs[o][:, columns] = part[o * chunk : (o + 1) * chunk]


def near(x):
    return pltpu.with_memory_space_constraint(x, pltpu.VMEM)


def local(doc_lengths, queries, keys, values, o_weight):
    n_ctx = lax.axis_size("ctx")
    n_kvh = lax.axis_size("kvh")
    groups = n_ctx // GROUP
    pair = pltpu.VMEM((2 * STRETCH, HEAD_WIDTH), BF)
    eight = pltpu.VMEM((GROUP, 2 * STRETCH, HEAD_WIDTH), BF)
    to_even, to_odd, own = pl.pallas_call(
        prep_kernel, out_shape=(pair, pair, eight), in_specs=[VMEM] * 2, out_specs=(VMEM,) * 3, name="prep"
    )(keys, values)

    def partner(i, odd):
        up = (i // GROUP) % 2 == odd
        if up and i >= n_ctx - GROUP:
            return 2 * n_ctx - GROUP - 1 - i
        return i + GROUP if up else i - GROUP

    def swap(x, odd):
        return lax.ppermute(x, "ctx", [(i, partner(i, odd)) for i in range(n_ctx) if partner(i, odd) >= 0])

    odd_in = swap(to_odd, 1)
    even_in = swap(to_even, 0)
    members = [list(range(g * GROUP, (g + 1) * GROUP)) for g in range(groups)]

    def exchange(x):
        return lax.all_to_all(x, "ctx", 0, 0, axis_index_groups=members, tiled=True)

    own = exchange(own)
    passed = pl.pallas_call(pass_kernel, out_shape=eight, in_specs=[VMEM] * 2, out_specs=VMEM, name="pass")(
        near(even_in), near(odd_in)
    )
    passed = exchange(passed)
    rows, inner = queries.shape
    width = o_weight.shape[1]
    keys_all = GROUP * STRETCH
    chunk = pltpu.VMEM((rows // n_kvh, width), BF)
    part = pl.pallas_call(
        lambda *refs: main_kernel(2 * n_ctx, doc_lengths.shape[0], *refs),
        out_shape=(chunk,) * n_kvh,
        in_specs=[VMEM] * 5 + [SMEM, pl.BlockSpec(memory_space=pl.ANY)],
        out_specs=(VMEM,) * n_kvh,
        scratch_shapes=[
            pltpu.VMEM((keys_all, HEAD_WIDTH), BF),
            pltpu.VMEM((keys_all, HEAD_WIDTH), BF),
            pltpu.VMEM((STRETCH, keys_all), F32),
            pltpu.VMEM((rows, inner), BF),
            pltpu.VMEM((rows, inner), BF),
            pltpu.VMEM(o_weight.shape, BF),
            pltpu.SemaphoreType.DMA,
        ],
        name="attend",
    )(queries, keys, values, own, near(passed), doc_lengths, o_weight)

    ring = list(range(0, n_kvh, 2)) + list(range(n_kvh - 1, 0, -2))
    onward = [(ring[i], ring[(i + 1) % n_kvh]) for i in range(n_kvh)]
    back = [(to, source) for source, to in onward]

    def add(a, b):
        return (a.astype(F32) + b.astype(F32)).astype(BF)

    far = n_kvh // 2
    a, b = part[far], part[far + 1]
    for step in range(far):
        a = lax.ppermute(a, "kvh", onward)
        if step < far - 1:
            b = lax.ppermute(b, "kvh", back)
            a = add(part[far - 1 - step], a)
            if step < far - 2:
                b = add(part[far + 2 + step], b)
    return (part[0].astype(F32) + a.astype(F32) + b.astype(F32)).astype(BF)


def solution(mesh):
    in_specs = (P(), P("ctx", "kvh"), P("ctx", "kvh"), P("ctx", "kvh"), P("kvh", None))
    out_specs = P(("ctx", "kvh"), None)
    return jax.shard_map(local, mesh=mesh, in_specs=in_specs, out_specs=out_specs, check_vma=False)
```

```python
import math

import jax
import jax.numpy as jnp
from jax import lax
from jax.experimental import pallas as pl
from jax.experimental.pallas import tpu as pltpu
from jax.sharding import PartitionSpec as P


BF = jnp.bfloat16
F32 = jnp.float32
HEAD_WIDTH = 128
STRETCH = 128
GROUP = 8
PAIR = 2
TILE = 512
NEG_FILL = -1e30
SCALE = math.log2(math.e) / math.sqrt(HEAD_WIDTH)
VMEM = pl.BlockSpec(memory_space=pltpu.VMEM)
SMEM = pl.BlockSpec(memory_space=pltpu.SMEM)


def prep_kernel(k_ref, v_ref, even_ref, odd_ref, own_ref):
    ctx = lax.axis_index("ctx")
    me = lax.rem(ctx, GROUP)
    is_odd = lax.rem(ctx // GROUP, 2) == 1

    def put(ref, at):
        ref[:STRETCH] = k_ref[at : at + STRETCH]
        ref[STRETCH:] = v_ref[at : at + STRETCH]

    @pl.when(is_odd)
    def _():
        put(odd_ref, 0)
        put(even_ref, STRETCH)

    @pl.when(jnp.logical_not(is_odd))
    def _():
        put(odd_ref, STRETCH)
        put(even_ref, 0)

    for j in range(GROUP):

        @pl.when(j >= me)
        def _():
            put(own_ref.at[j], 0)

        @pl.when(j < me)
        def _():
            put(own_ref.at[j], STRETCH)


def pass_kernel(even_ref, odd_ref, out_ref):
    ctx = lax.axis_index("ctx")
    me = lax.rem(ctx, GROUP)
    is_odd = lax.rem(ctx // GROUP, 2) == 1
    for j in range(GROUP):
        from_odd = (j >= me) == is_odd

        @pl.when(from_odd)
        def _():
            out_ref[j] = odd_ref[...]

        @pl.when(jnp.logical_not(from_odd))
        def _():
            out_ref[j] = even_ref[...]


def main_kernel(stretches, docs, q_ref, k_ref, v_ref, own_ref, sh_ref, len_ref, w_hbm, *rest):
    outs, (kbuf, vbuf, bias, attn, rows, wbuf, sem) = rest[:-7], rest[-7:]
    ctx = lax.axis_index("ctx")
    kvh = lax.axis_index("kvh")
    me = lax.rem(ctx, GROUP)
    group0 = ctx - me
    copy = pltpu.make_async_copy(w_hbm, wbuf, sem)
    copy.start()
    heads = q_ref.shape[1] // HEAD_WIDTH
    row = lax.broadcasted_iota(jnp.int32, (STRETCH, HEAD_WIDTH), 0)
    lane = lax.broadcasted_iota(jnp.int32, (STRETCH, HEAD_WIDTH), 1)
    for chain in range(2):
        q_base = (ctx if chain == 0 else stretches - 1 - ctx) * STRETCH
        q_place = q_base + row
        begin = jnp.zeros_like(row)
        end = jnp.int32(0)
        for n in range(docs):
            end = end + len_ref[n]
            begin = jnp.where(end <= q_place, end, begin)
        for s in range(GROUP):
            here = pl.ds(s * STRETCH, STRETCH)
            if chain == 0:
                near = s <= me
                source = group0 + s - jnp.where(near, 0, GROUP)
                key_base = source * STRETCH
            else:
                near = s >= me
                source = group0 + s + jnp.where(near, 0, GROUP)
                key_base = (stretches - 1 - source) * STRETCH

            @pl.when(near)
            def _():
                kbuf[here] = own_ref[s, :STRETCH]
                vbuf[here] = own_ref[s, STRETCH:]

            @pl.when(jnp.logical_not(near))
            def _():
                kbuf[here] = sh_ref[s, :STRETCH]
                vbuf[here] = sh_ref[s, STRETCH:]

            if chain == 1:
                @pl.when(s == me)
                def _():
                    kbuf[here] = k_ref[STRETCH:]
                    vbuf[here] = v_ref[STRETCH:]

            key_place = key_base + lane
            allowed = (key_place >= begin) & (key_place <= q_place)
            bias[:, here] = jnp.where(allowed, 0.0, NEG_FILL)
        mine = pl.ds(chain * STRETCH, STRETCH)
        stack = jnp.concatenate([q_ref[mine, h * HEAD_WIDTH : (h + 1) * HEAD_WIDTH] for h in range(heads)], axis=0)
        for g in range(0, heads, PAIR):
            many = stack[g * STRETCH : (g + PAIR) * STRETCH]
            scores = lax.dot_general(many, kbuf[...], (((1,), (1,)), ((), ())), preferred_element_type=F32)
            scores = scores.reshape(PAIR, STRETCH, GROUP * STRETCH) * SCALE + bias[...][None]
            highest = jnp.max(scores, axis=2, keepdims=True)
            weights = jnp.exp2(scores - highest)
            total = jnp.sum(weights, axis=2, keepdims=True)
            flat = weights.astype(BF).reshape(PAIR * STRETCH, GROUP * STRETCH)
            result = jnp.dot(flat, vbuf[...], preferred_element_type=F32).reshape(PAIR, STRETCH, HEAD_WIDTH)
            result = (result / total).astype(BF)
            for h in range(PAIR):
                attn[mine, (g + h) * HEAD_WIDTH : (g + h + 1) * HEAD_WIDTH] = result[h]
    n_kvh = len(outs)
    chunk = attn.shape[0] // n_kvh
    position = jnp.where(lax.rem(kvh, 2) == 0, kvh // 2, n_kvh - 1 - kvh // 2)
    for o in range(n_kvh):
        i = lax.rem(position + o, n_kvh)
        to = jnp.where(i < n_kvh // 2, 2 * i, 2 * n_kvh - 1 - 2 * i)
        rows[pl.ds(o * chunk, chunk)] = attn[pl.ds(pl.multiple_of(to * chunk, chunk), chunk)]
    copy.wait()
    for c in range(0, wbuf.shape[1], TILE):
        columns = pl.ds(c, TILE)
        part = jnp.dot(rows[...], wbuf[:, columns], preferred_element_type=F32).astype(BF)
        for o in range(n_kvh):
            outs[o][:, columns] = part[o * chunk : (o + 1) * chunk]


def near(x):
    return pltpu.with_memory_space_constraint(x, pltpu.VMEM)


def local(doc_lengths, queries, keys, values, o_weight):
    n_ctx = lax.axis_size("ctx")
    n_kvh = lax.axis_size("kvh")
    groups = n_ctx // GROUP
    pair = pltpu.VMEM((2 * STRETCH, HEAD_WIDTH), BF)
    eight = pltpu.VMEM((GROUP, 2 * STRETCH, HEAD_WIDTH), BF)
    to_even, to_odd, own = pl.pallas_call(
        prep_kernel, out_shape=(pair, pair, eight), in_specs=[VMEM] * 2, out_specs=(VMEM,) * 3, name="prep"
    )(keys, values)

    def partner(i, odd):
        up = (i // GROUP) % 2 == odd
        if up and i >= n_ctx - GROUP:
            return 2 * n_ctx - GROUP - 1 - i
        return i + GROUP if up else i - GROUP

    def swap(x, odd):
        return lax.ppermute(x, "ctx", [(i, partner(i, odd)) for i in range(n_ctx) if partner(i, odd) >= 0])

    odd_in = swap(to_odd, 1)
    even_in = swap(to_even, 0)
    members = [list(range(g * GROUP, (g + 1) * GROUP)) for g in range(groups)]

    def exchange(x):
        return lax.all_to_all(x, "ctx", 0, 0, axis_index_groups=members, tiled=True)

    own = exchange(own)
    passed = pl.pallas_call(pass_kernel, out_shape=eight, in_specs=[VMEM] * 2, out_specs=VMEM, name="pass")(
        near(even_in), near(odd_in)
    )
    passed = exchange(passed)
    rows, inner = queries.shape
    width = o_weight.shape[1]
    keys_all = GROUP * STRETCH
    chunk = pltpu.VMEM((rows // n_kvh, width), BF)
    part = pl.pallas_call(
        lambda *refs: main_kernel(2 * n_ctx, doc_lengths.shape[0], *refs),
        out_shape=(chunk,) * n_kvh,
        in_specs=[VMEM] * 5 + [SMEM, pl.BlockSpec(memory_space=pl.ANY)],
        out_specs=(VMEM,) * n_kvh,
        scratch_shapes=[
            pltpu.VMEM((keys_all, HEAD_WIDTH), BF),
            pltpu.VMEM((keys_all, HEAD_WIDTH), BF),
            pltpu.VMEM((STRETCH, keys_all), F32),
            pltpu.VMEM((rows, inner), BF),
            pltpu.VMEM((rows, inner), BF),
            pltpu.VMEM(o_weight.shape, BF),
            pltpu.SemaphoreType.DMA,
        ],
        name="attend",
    )(queries, keys, values, own, near(passed), doc_lengths, o_weight)

    ring = list(range(0, n_kvh, 2)) + list(range(n_kvh - 1, 0, -2))
    onward = [(ring[i], ring[(i + 1) % n_kvh]) for i in range(n_kvh)]
    back = [(to, source) for source, to in onward]

    def add(a, b):
        return (a.astype(F32) + b.astype(F32)).astype(BF)

    far = n_kvh // 2
    a, b = part[far], part[far + 1]
    for step in range(far):
        a = lax.ppermute(a, "kvh", onward)
        if step < far - 1:
            b = lax.ppermute(b, "kvh", back)
            a = add(part[far - 1 - step], a)
            if step < far - 2:
                b = add(part[far + 2 + step], b)
    return (part[0].astype(F32) + a.astype(F32) + b.astype(F32)).astype(BF)


def solution(mesh):
    in_specs = (P(), P("ctx", "kvh"), P("ctx", "kvh"), P("ctx", "kvh"), P("kvh", None))
    out_specs = P(("ctx", "kvh"), None)
    return jax.shard_map(local, mesh=mesh, in_specs=in_specs, out_specs=out_specs, check_vma=False)
```
